256 devices in a mesh: dp: 4 (over x), seq: 8 (over z), tensor: 8 (over y, core).
Axes of the slice: x: 4, y: 4, z: 8, core: 2. Of those that a mesh axis runs over, the one named last changes fastest.
Arguments:
- query_vectors: bfloat16 [1792, 4096], P(('dp', 'seq'), 'tensor'), may hold values from -128 to 128
- key_vectors: bfloat16 [1792, 2048], P(('dp', 'seq'), 'tensor'), may hold values from -6 to 6
- value_vectors: bfloat16 [1792, 2048], P(('dp', 'seq'), 'tensor'), may hold values from -6 to 6
- out_weight: bfloat16 [4096, 3584], P(None, 'tensor'), may hold values from -0.09375 to 0.09375
- residual: bfloat16 [1792, 3584], P(('dp', 'seq'), 'tensor'), may hold values from -64 to 64
- post_gain: float32 [3584], P('tensor'), may hold values from 0.1 to 1.9
- final_gain: float32 [3584], P('tensor'), may hold values from 0.1 to 1.9
- vocab_weight: bfloat16 [128000, 3584], P(('dp', 'seq', 'tensor')), may hold values from -4 to 4
- segment_ids: int32 [4, 448], P('dp', 'seq'), may hold values from 0 to 7, as said below
- doc_starts: int32 [4, 8], P('dp'), may hold values from 0 to 447, as said below
- doc_index: int32 [4, 8], P('dp'), may hold values from 0 to 31
- targets: int32 [4, 448], replicated, may hold values from 0 to 127999
Outputs:
- token_logprob: float32 [4, 448], P('dp', 'seq')
- doc_loglik: float32 [32], replicated
- doc_counts: float32 [32], replicated
The draws below stay inside these ranges and needn't reach their ends.
Inputs may be any that keep to these rules, and one draw needn't show every extreme that they name: `segment_ids`: within each row the numbers never fall and every number 0 to 7 appears; segment s of a row begins at doc_starts[row, s]; each segment holds 1 to 336 positions. doc_starts[row, 0] = 0 and the starts rise strictly along each row.
All inputs are finite; a program needn't handle non-finite values.
Results may differ from the reference program's by a relative error of at most 0.00074.
Values may be sent and summed in bfloat16 or wider, within the bound.
No kernel may reach another device: no remote copies, remote signals or barrier semaphores. Data moves between devices by JAX's collectives and lax.ppermute only.
A program may use at most 64 MiB of HBM per device.

```python
import math
import jax
import jax.numpy as jnp
import numpy as np
from jax import lax

D = 3584
HEADS = 16
KV_HEADS = 8
HEAD_DIM = 256
SEGS = 8
VOCAB = 128000
LENGTH = 448
ROWS = 4
TOKENS = 1792
MOSTDOC = 336
NDOCS = 32


def one_row(key):
    first_key, second_key = jax.random.split(key)
    leftover = LENGTH - MOSTDOC
    picks = jax.random.permutation(first_key, leftover - 1)[:SEGS - 2] + 1
    edges = jnp.concatenate([jnp.zeros((1,), jnp.int32), jnp.sort(picks).astype(jnp.int32), jnp.full((1,), leftover, jnp.int32)])
    others = edges[1:] - edges[:-1]
    padded = jnp.concatenate([others, jnp.zeros((1,), jnp.int32)])
    place = jax.random.randint(second_key, (), 0, SEGS)
    slots = jnp.arange(SEGS, dtype=jnp.int32)
    before = padded[slots]
    after = padded[jnp.maximum(slots - 1, 0)]
    return jnp.where(slots < place, before, jnp.where(slots == place, MOSTDOC, after)).astype(jnp.int32)


def document_layout(key):
    row_keys = jax.random.split(jax.random.fold_in(key, 17), ROWS)
    lengths = jax.vmap(one_row)(row_keys)
    starts = jnp.cumsum(lengths, axis=1) - lengths
    positions = jnp.arange(LENGTH, dtype=jnp.int32)
    segment_ids = jnp.sum((positions[None, :, None] >= starts[:, None, :]).astype(jnp.int32), axis=2) - 1
    return (segment_ids.astype(jnp.int32), starts.astype(jnp.int32))


def draw_segment_ids(key, part):
    return document_layout(key)[0]


def draw_doc_starts(key, part):
    return document_layout(key)[1]


def attention_inputs(key):
    base_key, noise_key, pick_key, strength_key, gap_key = jax.random.split(jax.random.fold_in(key, 41), 5)
    keys = jnp.clip(jax.random.normal(base_key, (TOKENS, KV_HEADS, HEAD_DIM)), -6.0, 6.0)
    noise = jnp.clip(jax.random.normal(noise_key, (TOKENS, HEADS, HEAD_DIM)), -6.0, 6.0)
    picked = (jax.random.randint(pick_key, (TOKENS, HEADS), 0, 8) == 0).astype(jnp.float32)
    strength = jnp.exp(jax.random.uniform(strength_key, (TOKENS, HEADS), minval=math.log(70.0 / 16.0), maxval=math.log(150.0 / 16.0)))
    gap = jax.random.uniform(gap_key, (TOKENS, HEADS), minval=15.0 / 16.0, maxval=40.0 / 16.0)
    group_size = HEADS // KV_HEADS
    own = jnp.repeat(keys, group_size, axis=1)
    prior = jnp.repeat(jnp.roll(keys, 1, axis=0), group_size, axis=1)
    lift = picked * strength
    second = picked * (strength - gap)
    queries = noise + lift[..., None] * own + second[..., None] * prior
    queries = jnp.clip(queries, -128.0, 128.0)
    return (queries.reshape(TOKENS, HEADS * HEAD_DIM), keys.reshape(TOKENS, KV_HEADS * HEAD_DIM))


def draw_query_vectors(key, part):
    return attention_inputs(key)[0].astype(jnp.bfloat16)


def draw_key_vectors(key, part):
    return attention_inputs(key)[1].astype(jnp.bfloat16)


def residual_keys(key):
    return jax.random.split(jax.random.fold_in(key, 29), 4)


def draw_residual(key, part):
    row_key, column_key, base_key, common_key = residual_keys(key)
    row_scale = jnp.exp(jax.random.uniform(row_key, (TOKENS, 1), minval=jnp.log(0.25), maxval=jnp.log(2.5)))
    column_scale = jnp.exp(jax.random.uniform(column_key, (1, D), minval=jnp.log(0.25), maxval=jnp.log(2.5)))
    base = jnp.clip(jax.random.normal(base_key, (TOKENS, D)), -6.0, 6.0)
    return (base * row_scale * column_scale).astype(jnp.bfloat16)


def draw_vocab_weight(key, part):
    base_key = jax.random.fold_in(jax.random.fold_in(key, 53), 0)
    spread = float(D // 9) ** (-0.5)
    weights = jnp.clip(jax.random.normal(base_key, (VOCAB, D)), -6.0, 6.0) * spread
    return weights.astype(jnp.bfloat16)


def with_ends(drawn, key, smallest, high):
    dims = drawn.shape
    spot = [jax.random.randint(jax.random.fold_in(key, axis), (), 0, dims[axis]) for axis in range(len(dims))]
    drawn = drawn.at[tuple(spot)].set(smallest)
    longest = dims.index(max(dims))
    spot[longest] = (spot[longest] + 1) % dims[longest]
    return drawn.at[tuple(spot)].set(high)


def steps_of(key, extent, pieces, smallest, top_value):
    loudness, own = 1.0, jax.random.fold_in(key, 6)
    for dim, blocks in pieces:
        heights = jnp.exp(jax.random.uniform(jax.random.fold_in(own, dim), (blocks,), jnp.float32, smallest / len(pieces), top_value / len(pieces)))
        loudness = loudness * jnp.repeat(heights, extent[dim] // blocks).reshape([-1 if axis == dim else 1 for axis in range(len(extent))])
    return loudness


def wide_ids(own_key, dims, number_of, lean):
    weights = [min(1 << octave, number_of + 1 - (1 << octave)) * (1 << 20) // math.isqrt((1 << octave) ** lean) + 1 for octave in range((number_of + 1).bit_length()) if 1 << octave <= number_of]
    deviation = 1 + sum(weights) // (1 << 30)
    grid = np.cumsum(np.array([max(1, weight // deviation) for weight in weights]))
    ticket = jax.random.randint(jax.random.fold_in(own_key, 1), dims, 0, int(grid[len(weights) - 1]))
    start = jnp.left_shift(1, jnp.searchsorted(jnp.asarray(grid, jnp.int32), ticket, side="right").astype(jnp.int32))
    grade = start - 1 + jax.random.randint(jax.random.fold_in(own_key, 4), dims, 0, 1 << 30) % jnp.minimum(start, number_of + 1 - start)
    return jax.random.permutation(jax.random.fold_in(own_key, 2), number_of)[grade].astype(jnp.int32)


def centred(rng, shape, scale, bound, pieces=(), kind=jnp.bfloat16):
    values = jax.random.normal(rng, shape, jnp.float32) * scale
    if len(pieces) > 0:
        values = steps_of(rng, shape, pieces, -0.22, 0.18) * values
    return jnp.clip(values, min=-bound, max=bound).astype(kind)


def setup_inputs(seed: int = 0) -> dict:
    streams_of = jax.random.split(jax.random.key(seed), 13)
    return {
        "query_vectors": draw_query_vectors(jax.random.fold_in(streams_of[12], 71), 0),
        "key_vectors": draw_key_vectors(jax.random.fold_in(streams_of[12], 71), 0),
        "value_vectors": centred(streams_of[2], (TOKENS, KV_HEADS * HEAD_DIM), 1.0, 6.0, ((0, 32), (1, 8))),
        "out_weight": centred(streams_of[3], (HEADS * HEAD_DIM, D), (HEADS * HEAD_DIM) ** -0.5, 0.09375, ((1, 8),)),
        "residual": draw_residual(jax.random.fold_in(streams_of[12], 71), 0),
        "post_gain": jnp.clip(1.0 + 0.18 * jax.random.normal(streams_of[5], (D,), jnp.float32), 0.1, 1.9),
        "final_gain": jnp.clip(1.0 + 0.18 * jax.random.normal(streams_of[6], (D,), jnp.float32), 0.1, 1.9),
        "vocab_weight": draw_vocab_weight(jax.random.fold_in(streams_of[12], 71), 0),
        "segment_ids": draw_segment_ids(jax.random.fold_in(streams_of[12], 71), 0),
        "doc_starts": draw_doc_starts(jax.random.fold_in(streams_of[12], 71), 0),
        "doc_index": with_ends(jax.random.randint(streams_of[10], (ROWS, SEGS), 0, NDOCS), jax.random.fold_in(streams_of[10], 1), 0, NDOCS - 1).astype(jnp.int32),
        "targets": with_ends(wide_ids(streams_of[11], (ROWS, LENGTH), VOCAB, 2), jax.random.fold_in(streams_of[11], 3), 0, VOCAB - 1).astype(jnp.int32),
    }


ATTENTION_CAP = 50.0
LOGIT_CAP = 30.0
EPSILON = 1e-06

def first_positions(segment_row, start_row):
    segment_match = segment_row[:, None] == jnp.arange(SEGS, dtype=jnp.int32)[None, :]
    return lax.optimization_barrier(jnp.sum(jnp.where(segment_match, start_row[None, :], 0), axis=1)).astype(jnp.int32)

def attend_row(inputs):
    query_row, key_row, value_row, segment_row, start_row = inputs
    group_size = HEADS // KV_HEADS
    query_heads = query_row.astype(jnp.float32).reshape(LENGTH, KV_HEADS, group_size, HEAD_DIM)
    key_heads = key_row.astype(jnp.float32).reshape(LENGTH, KV_HEADS, HEAD_DIM)
    value_heads = value_row.astype(jnp.float32).reshape(LENGTH, KV_HEADS, HEAD_DIM)
    raw_scores = jnp.einsum('ikgd,jkd->ikgj', query_heads, key_heads)
    capped = ATTENTION_CAP * jnp.tanh(raw_scores * HEAD_DIM ** (-0.5) / ATTENTION_CAP)
    positions = jnp.arange(LENGTH, dtype=jnp.int32)
    doc_first = first_positions(segment_row, start_row)
    visible = (positions[None, :] <= positions[:, None]) & (positions[None, :] >= doc_first[:, None])
    weights = jnp.where(visible[:, None, None, :], jnp.exp(capped), 0.0)
    denominator = lax.optimization_barrier(jnp.sum(weights, axis=-1))
    rounded = lax.optimization_barrier(weights.astype(jnp.bfloat16)).astype(jnp.float32)
    numerator = jnp.einsum('ikgj,jkd->ikgd', rounded, value_heads)
    attended = numerator / denominator[..., None]
    return attended.reshape(LENGTH, HEADS * HEAD_DIM).astype(jnp.bfloat16)

def reference(query_vectors, key_vectors, value_vectors, out_weight, residual, post_gain, final_gain, vocab_weight, segment_ids, doc_starts, doc_index, targets):
    attended = lax.map(attend_row, (query_vectors.reshape(ROWS, LENGTH, HEADS * HEAD_DIM), key_vectors.reshape(ROWS, LENGTH, KV_HEADS * HEAD_DIM), value_vectors.reshape(ROWS, LENGTH, KV_HEADS * HEAD_DIM), segment_ids, doc_starts))
    attended = attended.reshape(TOKENS, HEADS * HEAD_DIM)
    branch = jnp.dot(attended, out_weight, preferred_element_type=jnp.float32)
    branch_rms = jnp.sqrt(lax.optimization_barrier(jnp.mean(branch * branch, axis=1, keepdims=True)) + EPSILON)
    updated = residual.astype(jnp.float32) + post_gain[None, :] * branch / branch_rms
    updated_rms = jnp.sqrt(lax.optimization_barrier(jnp.mean(updated * updated, axis=1, keepdims=True)) + EPSILON)
    hidden = (final_gain[None, :] * updated / updated_rms).astype(jnp.bfloat16)
    block_rows = math.gcd(TOKENS, 256)

    def head_block(inputs):
        rows_in, label_rows = inputs
        logits = lax.dot_general(rows_in, vocab_weight, (((1,), (1,)), ((), ())), preferred_element_type=jnp.float32)
        capped = LOGIT_CAP * jnp.tanh(logits / LOGIT_CAP)
        totals = lax.optimization_barrier(jnp.sum(jnp.exp(capped), axis=1))
        chosen = jnp.take_along_axis(capped, label_rows[:, None], axis=1)[:, 0]
        return (totals, chosen)
    totals, chosen = lax.map(head_block, (hidden.reshape(TOKENS // block_rows, block_rows, D), targets.reshape(TOKENS // block_rows, block_rows)))
    totals = totals.reshape(ROWS, LENGTH)
    chosen = chosen.reshape(ROWS, LENGTH)
    positions = jnp.arange(LENGTH, dtype=jnp.int32)
    segment_slots = jnp.arange(SEGS, dtype=jnp.int32)
    next_segment = segment_ids + 1
    doc_end = lax.optimization_barrier(jnp.sum(jnp.where(segment_slots[None, None, :] == next_segment[:, :, None], doc_starts[:, None, :], 0), axis=2))
    doc_end = doc_end + jnp.where(next_segment == SEGS, LENGTH, 0)
    counted = (positions[None, :] + 1 < doc_end).astype(jnp.float32)
    token_logprob = counted * (chosen - jnp.log(totals))
    doc_of = lax.optimization_barrier(jnp.sum(jnp.where(segment_slots[None, None, :] == segment_ids[:, :, None], doc_index[:, None, :], 0), axis=2))
    doc_match = (doc_of.reshape(TOKENS)[:, None] == jnp.arange(NDOCS, dtype=jnp.int32)[None, :]).astype(jnp.float32)
    doc_loglik = lax.optimization_barrier(jnp.sum(token_logprob.reshape(TOKENS)[:, None] * doc_match, axis=0))
    doc_counts = lax.optimization_barrier(jnp.sum(counted.reshape(TOKENS)[:, None] * doc_match, axis=0))
    return (token_logprob, doc_loglik, doc_counts)
```

```python
import jax
import jax.numpy as jnp
from jax import lax
from jax.sharding import Mesh
from jax.sharding import PartitionSpec as P

D = 3584
HEAD_DIM = 256
TENSOR = ("tensor_0", "tensor_1")
DP_SEQ_TENSOR = ("dp", "seq", "tensor_0", "tensor_1")


ATTENTION_CAP = 50.0
LOGIT_CAP = 30.0
EPSILON = 1e-06


def side_by_side(arrays, axis, dim, along):
    ends, at = ([], 0)
    for a in arrays[:-1]:
        at += a.shape[along]
        ends.append(at)
    both = jnp.concatenate(arrays, axis=along)
    return tuple(jnp.split(lax.all_gather(both, axis, axis=dim, tiled=True), ends, axis=along))


def laid_out(blocks, dim):
    blocks = jnp.moveaxis(blocks, 0, dim)
    lengths = blocks.shape
    return blocks.reshape(*lengths[:dim], lengths[dim] * lengths[dim + 1], *lengths[dim + 2 :])


def copy_for_each(shard, axis):
    size = lax.axis_size(axis)
    return lax.all_to_all(
        jnp.broadcast_to(shard[None], (size, *shard.shape)), axis, 0, 0, tiled=True
    )


def collect(shard, axis, dim):
    return laid_out(copy_for_each(shard, axis), dim)


def over_copies(shard, axis):
    return copy_for_each(shard, axis).sum(axis=0)


def together(arrays, axis):
    ends = [0]
    for a in arrays:
        ends.append(ends[-1] + a.size)
    total = over_copies(jnp.concatenate([a.ravel() for a in arrays]), axis)
    return tuple((total[b:e].reshape(a.shape) for a, b, e in zip(arrays, ends, ends[1:])))


def swapped(x):
    return lax.ppermute(x, "tensor_1", [(0, 1), (1, 0)])


def along_x(x, step):
    size = lax.axis_size("dp")
    return lax.ppermute(x, "dp", [(i, (i + step) % size) for i in range(size)])


def shared_vocabulary(vocab_weight):
    count = vocab_weight.shape[0]
    cut = count // 16 * 8 + 8
    dp_size, seq_size = lax.axis_size("dp"), lax.axis_size("seq")
    tensor_size = lax.axis_size(TENSOR)
    dp, seq = lax.axis_index("dp"), lax.axis_index("seq")
    place, core = lax.axis_index(TENSOR), lax.axis_index("tensor_1")
    partner = place + 1 - 2 * core

    def first(chip_x, slot):
        return ((chip_x % dp_size * seq_size + seq) * tensor_size + slot) * count

    from_left = along_x(vocab_weight[:cut], 1)
    from_right = along_x(vocab_weight[cut:], -1)
    left, right = dp + dp_size - 1, dp + 1
    return (
        (vocab_weight, first(dp, place)),
        (swapped(vocab_weight), first(dp, partner)),
        (from_left, first(left, place)),
        (swapped(from_left), first(left, partner)),
        (from_right, first(right, place) + cut),
        (swapped(from_right), first(right, partner) + cut),
    )


def row_features(hidden, on_first):
    size = lax.axis_size("dp")
    same, cross = [], []
    for x in range(size):
        after, before = (x + 1) % size, (x - 1) % size
        same += [(2 * x, 2 * before), (2 * x + 1, 2 * after + 1)]
        cross += [(2 * x, 2 * after + 1), (2 * x + 1, 2 * before)]
    a = lax.ppermute(hidden, ("dp", "tensor_1"), same)
    b = lax.ppermute(hidden, ("dp", "tensor_1"), cross)
    return jnp.concatenate([jnp.where(on_first, a, b), jnp.where(on_first, b, a)], axis=1)


def vocabulary_sums(piece, block_in, labels, first_id):
    logits = lax.dot_general(
        piece, block_in, (((1,), (1,)), ((), ())), preferred_element_type=jnp.float32
    )
    capped = LOGIT_CAP * jnp.tanh(logits / LOGIT_CAP)
    ids = first_id + jnp.arange(piece.shape[0], dtype=jnp.int32)
    totals = jnp.sum(jnp.exp(capped), axis=0)
    chosen = jnp.sum(jnp.where(ids[:, None] == labels[None, :], capped, 0.0), axis=0)
    return totals, chosen


def local(
    query_vectors,
    key_vectors,
    value_vectors,
    out_weight,
    residual,
    post_gain,
    final_gain,
    vocab_weight,
    segment_ids,
    doc_starts,
    doc_index,
    targets,
):
    tok_rows = query_vectors.shape[0]
    seg_row = segment_ids[0]
    starts = doc_starts[0]
    seg_count = starts.shape[0]
    slot_ids = jnp.arange(seg_count, dtype=jnp.int32)
    positions = lax.axis_index("seq") * tok_rows + jnp.arange(tok_rows, dtype=jnp.int32)
    doc_first = jnp.sum(
        jnp.where(seg_row[:, None] == slot_ids[None, :], starts[None, :], 0), axis=1
    )
    local_groups = key_vectors.shape[1] // HEAD_DIM
    group_size = query_vectors.shape[1] // key_vectors.shape[1]
    query_heads = query_vectors.reshape(tok_rows, local_groups, group_size, HEAD_DIM)
    score_scale = HEAD_DIM ** (-0.5)
    weight_pieces = shared_vocabulary(vocab_weight)
    kv_width = key_vectors.shape[1]
    both = collect(jnp.concatenate((key_vectors, value_vectors), axis=1), "seq", 0)
    key_block, value_block = both[:, :kv_width], both[:, kv_width:]
    row_count = key_block.shape[0]
    key_heads = key_block.reshape(row_count, local_groups, HEAD_DIM)
    value_heads = value_block.reshape(row_count, local_groups, HEAD_DIM)
    raw_scores = jnp.einsum(
        "ikgd,jkd->ikgj", query_heads, key_heads, preferred_element_type=jnp.float32
    )
    capped = ATTENTION_CAP * jnp.tanh(raw_scores * score_scale / ATTENTION_CAP)
    key_positions = jnp.arange(row_count, dtype=jnp.int32)
    visible = (key_positions[None, :] <= positions[:, None]) & (
        key_positions[None, :] >= doc_first[:, None]
    )
    weights = jnp.where(visible[:, None, None, :], jnp.exp(capped), 0.0)
    rounded = weights.astype(jnp.bfloat16)
    numerator = jnp.einsum(
        "ikgj,jkd->ikgd", rounded, value_heads, preferred_element_type=jnp.float32
    )
    denominator = jnp.sum(weights, axis=-1)
    numerator, denominator = (numerator, denominator)
    attended = (
        (numerator / denominator[..., None])
        .reshape(tok_rows, query_vectors.shape[1])
        .astype(jnp.bfloat16)
    )
    branch = jnp.dot(collect(attended, TENSOR, 1), out_weight, preferred_element_type=jnp.float32)
    carried_in = residual.astype(jnp.float32)
    gained = post_gain[None, :] * branch
    sq_branch, sq_carried, cross_sum, sq_gained = together(
        (
            jnp.sum(branch * branch, axis=1),
            jnp.sum(carried_in * carried_in, axis=1),
            jnp.sum(carried_in * gained, axis=1),
            jnp.sum(gained * gained, axis=1),
        ),
        TENSOR,
    )
    inv_branch = 1.0 / jnp.sqrt(sq_branch / D + EPSILON)
    updated = carried_in + gained * inv_branch[:, None]
    sq_total = sq_carried + 2.0 * inv_branch * cross_sum + inv_branch * inv_branch * sq_gained
    hidden = (final_gain[None, :] * updated / jnp.sqrt(sq_total / D + EPSILON)[:, None]).astype(
        jnp.bfloat16
    )
    dp_size = lax.axis_size("dp")
    seq_size = lax.axis_size("seq")
    row_len = tok_rows * seq_size
    on_first = lax.axis_index("tensor_1") == 0
    taken_row = (lax.axis_index("dp") + jnp.where(on_first, 1, dp_size - 1)) % dp_size
    features = collect(row_features(hidden, on_first), "tensor_0", 1)
    block_in = lax.all_gather(features, "seq", axis=0, tiled=True)
    labels = lax.dynamic_index_in_dim(targets, taken_row, 0, keepdims=False)
    totals = jnp.zeros((row_len,), jnp.float32)
    chosen = jnp.zeros((row_len,), jnp.float32)
    for piece, first_id in weight_pieces:
        part_total, part_chosen = vocabulary_sums(piece, block_in, labels, first_id)
        totals, chosen = totals + part_total, chosen + part_chosen
    tile = (8, 128)
    spare = jnp.zeros((tile[0] * tile[1] - 2 * row_len,), jnp.float32)
    sums = over_copies(jnp.concatenate([totals, chosen, spare]).reshape(tile), "tensor_0").ravel()
    spare = jnp.zeros((tile[0] * tile[1] - 2 * row_len - 2 * seg_count,), jnp.float32)
    packed = jnp.concatenate(
        [
            sums[: 2 * row_len],
            starts.astype(jnp.float32),
            doc_index[0].astype(jnp.float32),
            spare,
        ]
    )
    arrived = copy_for_each(packed.reshape(tile), ("dp", "seq"))
    arrived = arrived.reshape(dp_size, seq_size, tile[0] * tile[1])
    own = jnp.sum(arrived[:, :, : 2 * row_len], axis=1)
    segments = arrived[:, 0, 2 * row_len : 2 * row_len + 2 * seg_count].astype(jnp.int32)
    other = lax.ppermute(own, "tensor_1", [(0, 1), (1, 0)])
    below, above = jnp.where(on_first, own, other), jnp.where(on_first, other, own)
    complete = jnp.roll(below, 1, axis=0) + jnp.roll(above, -1, axis=0)
    totals, chosen = complete[:, :row_len], complete[:, row_len:]
    all_starts, all_docs = segments[:, :seg_count], segments[:, seg_count:]
    places = jnp.arange(row_len, dtype=jnp.int32)
    ends = jnp.concatenate(
        [all_starts[:, 1:], jnp.full((dp_size, 1), row_len, jnp.int32)], axis=1
    )
    inside = (places[None, None, :] >= all_starts[:, :, None]) & (
        places[None, None, :] < ends[:, :, None]
    )
    last = jnp.sum(jnp.where(inside, ends[:, :, None], 0), axis=1)
    counted = (places[None, :] + 1 < last).astype(jnp.float32)
    logprob = counted * (chosen - jnp.log(totals))
    seg_loglik = jnp.sum(jnp.where(inside, logprob[:, None, :], 0.0), axis=2)
    seg_counts = jnp.sum(jnp.where(inside, counted[:, None, :], 0.0), axis=2)
    doc_total = seg_count * dp_size
    doc_match = all_docs[None, :, :] == jnp.arange(doc_total, dtype=jnp.int32)[:, None, None]
    doc_loglik = jnp.sum(jnp.where(doc_match, seg_loglik[None], 0.0), axis=(1, 2))
    doc_counts = jnp.sum(jnp.where(doc_match, seg_counts[None], 0.0), axis=(1, 2))
    token_logprob = lax.dynamic_slice(
        logprob, (lax.axis_index("dp"), lax.axis_index("seq") * tok_rows), (1, tok_rows)
    )
    return (token_logprob, doc_loglik, doc_counts)


def solution(mesh):
    split = Mesh(
        mesh.devices.reshape(mesh.shape["dp"], mesh.shape["seq"], 4, 2),
        ("dp", "seq", "tensor_0", "tensor_1"),
    )
    in_specs = (
        P(("dp", "seq"), TENSOR),
        P(("dp", "seq"), TENSOR),
        P(("dp", "seq"), TENSOR),
        P(None, TENSOR),
        P(("dp", "seq"), TENSOR),
        P(TENSOR),
        P(TENSOR),
        P(DP_SEQ_TENSOR, None),
        P("dp", "seq"),
        P("dp", None),
        P("dp", None),
        P(),
    )
    out_specs = (P("dp", "seq"), P(), P())
    return jax.shard_map(local, mesh=split, in_specs=in_specs, out_specs=out_specs, check_vma=False)
```

```python
import functools

import jax
import jax.numpy as jnp
from jax import lax
from jax.experimental import pallas as pl
from jax.experimental.pallas import tpu as pltpu
from jax.sharding import Mesh
from jax.sharding import PartitionSpec as P

D = 3584
HEAD_DIM = 256
TENSOR = ("tensor_0", "tensor_1")
DP_SEQ_TENSOR = ("dp", "seq", "tensor_0", "tensor_1")


ATTENTION_CAP = 50.0
LOGIT_CAP = 30.0
EPSILON = 1e-06


def side_by_side(arrays, axis, dim, along):
    ends, at = ([], 0)
    for a in arrays[:-1]:
        at += a.shape[along]
        ends.append(at)
    both = jnp.concatenate(arrays, axis=along)
    return tuple(jnp.split(lax.all_gather(both, axis, axis=dim, tiled=True), ends, axis=along))


def laid_out(blocks, dim):
    blocks = jnp.moveaxis(blocks, 0, dim)
    lengths = blocks.shape
    return blocks.reshape(*lengths[:dim], lengths[dim] * lengths[dim + 1], *lengths[dim + 2 :])


def copy_for_each(shard, axis):
    size = lax.axis_size(axis)
    return lax.all_to_all(
        jnp.broadcast_to(shard[None], (size, *shard.shape)), axis, 0, 0, tiled=True
    )


def collect(shard, axis, dim):
    return laid_out(copy_for_each(shard, axis), dim)


def over_copies(shard, axis):
    return copy_for_each(shard, axis).sum(axis=0)


def together(arrays, axis):
    ends = [0]
    for a in arrays:
        ends.append(ends[-1] + a.size)
    total = over_copies(jnp.concatenate([a.ravel() for a in arrays]), axis)
    return tuple((total[b:e].reshape(a.shape) for a, b, e in zip(arrays, ends, ends[1:])))


def swapped(x):
    return lax.ppermute(x, "tensor_1", [(0, 1), (1, 0)])


def shared_vocabulary(vocab_weight):
    count = vocab_weight.shape[0]
    size, seq_size = lax.axis_size("dp"), lax.axis_size("seq")
    tensor_size = lax.axis_size(TENSOR)
    dp, seq = lax.axis_index("dp"), lax.axis_index("seq")
    place, core = lax.axis_index(TENSOR), lax.axis_index("tensor_1")
    partner = place + 1 - 2 * core
    outward = []
    for x in range(size):
        outward += [(2 * x, 2 * ((x + 1) % size)), (2 * x + 1, 2 * ((x - 1) % size) + 1)]
    near = lax.ppermute(vocab_weight, ("dp", "tensor_1"), outward)

    def first(chip_x, slot):
        return ((chip_x % size * seq_size + seq) * tensor_size + slot) * count

    mine = dp + jnp.where(core == 0, size - 1, 1)
    other = dp + jnp.where(core == 0, 1, size - 1)
    firsts = (first(dp, place), first(dp, partner), first(mine, place), first(other, partner))
    return vocab_weight, swapped(vocab_weight), near, jnp.stack(firsts)


def row_features(hidden, on_first):
    size = lax.axis_size("dp")
    same, cross = [], []
    for x in range(size):
        after, before = (x + 1) % size, (x - 1) % size
        same += [(2 * x, 2 * before), (2 * x + 1, 2 * after + 1)]
        cross += [(2 * x, 2 * after + 1), (2 * x + 1, 2 * before)]
    a = lax.ppermute(hidden, ("dp", "tensor_1"), same)
    b = lax.ppermute(hidden, ("dp", "tensor_1"), cross)
    return jnp.concatenate([jnp.where(on_first, a, b), jnp.where(on_first, b, a)], axis=1)


def ring_step(below, above, axis):
    size = lax.axis_size(axis)
    up = [(i, (i + 1) % size) for i in range(size)]
    down = [(i, (i - 1) % size) for i in range(size)]
    return lax.ppermute(below, axis, up), lax.ppermute(above, axis, down)


def vocabulary_kernel(sizes, counts, first_ref, labels_ref, *refs):
    blocks, weights = refs[: len(sizes)], refs[len(sizes) : len(sizes) + len(counts)]
    out_ref, tokens = refs[len(sizes) + len(counts) :][:2]
    held = refs[len(sizes) + len(counts) + 2 :][: len(counts)]
    token_sems, weight_sems = refs[-2:]
    loads, at = [], 0
    for i, size in enumerate(sizes):
        loads.append(
            pltpu.make_async_copy(blocks[i], tokens.at[pl.ds(at, size)], token_sems.at[i])
        )
        at += size
    fills = [
        pltpu.make_async_copy(w, h, weight_sems.at[i]) for i, (w, h) in enumerate(zip(weights, held))
    ]
    for load in loads:
        load.start()
    fills[0].start()
    for load in loads:
        load.wait()
    fills[1].start()
    totals = jnp.zeros((1, at), jnp.float32)
    chosen = jnp.zeros((1, at), jnp.float32)
    for i, count in enumerate(counts):
        fills[i].wait()
        if i + 2 < len(counts):
            fills[i + 2].start()
        cut = count // 16 * 8 + 8
        for begin, rows in ((0, cut), (cut, count - cut)):
            logits = lax.dot_general(
                held[i][pl.ds(begin, rows), :],
                tokens[...],
                (((1,), (1,)), ((), ())),
                preferred_element_type=jnp.float32,
            )
            capped = LOGIT_CAP * jnp.tanh(logits / LOGIT_CAP)
            ids = first_ref[i] + begin + lax.broadcasted_iota(jnp.int32, (rows, at), 0)
            totals += jnp.sum(jnp.exp(capped), axis=0, keepdims=True)
            match = ids == labels_ref[...]
            chosen += jnp.sum(jnp.where(match, capped, 0.0), axis=0, keepdims=True)
    out_ref[0:1, :] = totals
    out_ref[1:2, :] = chosen


def vocabulary_sums(blocks, labels, weights, firsts):
    sizes = tuple(b.shape[0] for b in blocks)
    counts = tuple(w.shape[0] for w in weights)
    tokens, depth = sum(sizes), blocks[0].shape[1]
    in_place = pl.BlockSpec(memory_space=pl.ANY)
    work = tokens * depth * sum(counts)
    return pl.pallas_call(
        functools.partial(vocabulary_kernel, sizes, counts),
        out_shape=jax.ShapeDtypeStruct((2, tokens), jnp.float32),
        in_specs=[
            pl.BlockSpec(memory_space=pltpu.SMEM),
            pl.BlockSpec(memory_space=pltpu.VMEM),
            *[in_place] * (len(sizes) + len(counts)),
        ],
        out_specs=pl.BlockSpec(memory_space=pltpu.VMEM),
        scratch_shapes=[
            pltpu.VMEM((tokens, depth), blocks[0].dtype),
            *[pltpu.VMEM(w.shape, w.dtype) for w in weights],
            pltpu.SemaphoreType.DMA((len(sizes),)),
            pltpu.SemaphoreType.DMA((len(counts),)),
        ],
        compiler_params=pltpu.CompilerParams(vmem_limit_bytes=28 * 2**20),
        cost_estimate=pl.CostEstimate(
            flops=2 * work,
            transcendentals=2 * tokens * sum(counts),
            bytes_accessed=2 * depth * (tokens + sum(counts)),
        ),
        name="vocabulary_sums",
    )(firsts, labels, *blocks, *weights)


def local(
    query_vectors,
    key_vectors,
    value_vectors,
    out_weight,
    residual,
    post_gain,
    final_gain,
    vocab_weight,
    segment_ids,
    doc_starts,
    doc_index,
    targets,
):
    tok_rows = query_vectors.shape[0]
    seg_row = segment_ids[0]
    starts = doc_starts[0]
    seg_count = starts.shape[0]
    slot_ids = jnp.arange(seg_count, dtype=jnp.int32)
    positions = lax.axis_index("seq") * tok_rows + jnp.arange(tok_rows, dtype=jnp.int32)
    doc_first = jnp.sum(
        jnp.where(seg_row[:, None] == slot_ids[None, :], starts[None, :], 0), axis=1
    )
    local_groups = key_vectors.shape[1] // HEAD_DIM
    group_size = query_vectors.shape[1] // key_vectors.shape[1]
    query_heads = query_vectors.reshape(tok_rows, local_groups, group_size, HEAD_DIM)
    score_scale = HEAD_DIM ** (-0.5)
    own_entries, chip_entries, near_entries, firsts = shared_vocabulary(vocab_weight)
    kv_width = key_vectors.shape[1]
    both = collect(jnp.concatenate((key_vectors, value_vectors), axis=1), "seq", 0)
    key_block, value_block = both[:, :kv_width], both[:, kv_width:]
    row_count = key_block.shape[0]
    key_heads = key_block.reshape(row_count, local_groups, HEAD_DIM)
    value_heads = value_block.reshape(row_count, local_groups, HEAD_DIM)
    raw_scores = jnp.einsum(
        "ikgd,jkd->ikgj", query_heads, key_heads, preferred_element_type=jnp.float32
    )
    capped = ATTENTION_CAP * jnp.tanh(raw_scores * score_scale / ATTENTION_CAP)
    key_positions = jnp.arange(row_count, dtype=jnp.int32)
    visible = (key_positions[None, :] <= positions[:, None]) & (
        key_positions[None, :] >= doc_first[:, None]
    )
    weights = jnp.where(visible[:, None, None, :], jnp.exp(capped), 0.0)
    rounded = weights.astype(jnp.bfloat16)
    numerator = jnp.einsum(
        "ikgj,jkd->ikgd", rounded, value_heads, preferred_element_type=jnp.float32
    )
    denominator = jnp.sum(weights, axis=-1)
    numerator, denominator = (numerator, denominator)
    attended = (
        (numerator / denominator[..., None])
        .reshape(tok_rows, query_vectors.shape[1])
        .astype(jnp.bfloat16)
    )
    heads = collect(attended, TENSOR, 1)
    heads, near_entries = lax.optimization_barrier((heads, near_entries))
    far_entries = swapped(near_entries)
    branch = jnp.dot(heads, out_weight, preferred_element_type=jnp.float32)
    carried_in = residual.astype(jnp.float32)
    gained = post_gain[None, :] * branch
    sq_branch, sq_carried, cross_sum, sq_gained = together(
        (
            jnp.sum(branch * branch, axis=1),
            jnp.sum(carried_in * carried_in, axis=1),
            jnp.sum(carried_in * gained, axis=1),
            jnp.sum(gained * gained, axis=1),
        ),
        TENSOR,
    )
    inv_branch = 1.0 / jnp.sqrt(sq_branch / D + EPSILON)
    updated = carried_in + gained * inv_branch[:, None]
    sq_total = sq_carried + 2.0 * inv_branch * cross_sum + inv_branch * inv_branch * sq_gained
    hidden = (final_gain[None, :] * updated / jnp.sqrt(sq_total / D + EPSILON)[:, None]).astype(
        jnp.bfloat16
    )
    dp_size = lax.axis_size("dp")
    seq_size = lax.axis_size("seq")
    row_len = tok_rows * seq_size
    on_first = lax.axis_index("tensor_1") == 0
    taken_row = (lax.axis_index("dp") + jnp.where(on_first, 1, dp_size - 1)) % dp_size
    features = collect(row_features(hidden, on_first), "tensor_0", 1)
    entries = (own_entries, chip_entries, near_entries, far_entries)
    features, entries = lax.optimization_barrier((features, entries))
    entries = [pltpu.with_memory_space_constraint(w, pltpu.HBM) for w in entries]
    labels = lax.dynamic_index_in_dim(targets, taken_row, 0, keepdims=False)
    seq_start = lax.axis_index("seq") * tok_rows
    labels = lax.dynamic_slice_in_dim(jnp.concatenate([labels, labels]), seq_start, row_len)
    below, above = [features], [features]
    for _ in range(seq_size // 2 - 2):
        below_next, above_next = ring_step(below[-1], above[-1], "seq")
        below.append(below_next)
        above.append(above_next)
    far = len(above)
    near_labels = jnp.concatenate([labels[: far * tok_rows], labels[row_len - (far - 1) * tok_rows :]])
    far_labels = labels[far * tok_rows : row_len - (far - 1) * tok_rows]
    near_sums = vocabulary_sums(above + below[:0:-1], near_labels[None], entries, firsts)
    last_below, last_above = ring_step(below[-1], above[-1], "seq")
    last_below, last_above, near_sums = lax.optimization_barrier(
        (last_below, last_above, near_sums)
    )
    cut = tok_rows // 16 * 8 + 8
    head, tail = ring_step(last_below[:cut], last_above[cut:], "seq")
    far_sums = vocabulary_sums([last_above, head, tail, last_below], far_labels[None], entries, firsts)
    ahead = jnp.concatenate(
        [near_sums[:, : far * tok_rows], far_sums, near_sums[:, far * tok_rows :]] * 2, axis=1
    )
    in_order = lax.dynamic_slice_in_dim(ahead, row_len - seq_start, row_len, axis=1)
    by_place = copy_for_each(in_order, TENSOR)
    by_core = jnp.sum(by_place.reshape(-1, 2, 2 * row_len), axis=0)
    tile = (16, 128)
    spare = jnp.zeros((tile[0] * tile[1] - 4 * row_len - 2 * seg_count,), jnp.float32)
    packed = jnp.concatenate(
        [
            by_core.ravel(),
            starts.astype(jnp.float32),
            doc_index[0].astype(jnp.float32),
            spare,
        ]
    )
    arrived = copy_for_each(packed.reshape(tile), ("dp", "seq"))
    arrived = arrived.reshape(dp_size, seq_size, tile[0] * tile[1])
    by_chip = jnp.sum(arrived[:, :, : 4 * row_len], axis=1)
    segments = arrived[:, 0, 4 * row_len : 4 * row_len + 2 * seg_count].astype(jnp.int32)
    below, above = by_chip[:, : 2 * row_len], by_chip[:, 2 * row_len :]
    complete = jnp.roll(below, 1, axis=0) + jnp.roll(above, -1, axis=0)
    totals, chosen = complete[:, :row_len], complete[:, row_len:]
    all_starts, all_docs = segments[:, :seg_count], segments[:, seg_count:]
    places = jnp.arange(row_len, dtype=jnp.int32)
    ends = jnp.concatenate(
        [all_starts[:, 1:], jnp.full((dp_size, 1), row_len, jnp.int32)], axis=1
    )
    inside = (places[None, None, :] >= all_starts[:, :, None]) & (
        places[None, None, :] < ends[:, :, None]
    )
    last = jnp.sum(jnp.where(inside, ends[:, :, None], 0), axis=1)
    counted = (places[None, :] + 1 < last).astype(jnp.float32)
    logprob = counted * (chosen - jnp.log(totals))
    seg_loglik = jnp.sum(jnp.where(inside, logprob[:, None, :], 0.0), axis=2)
    seg_counts = jnp.sum(jnp.where(inside, counted[:, None, :], 0.0), axis=2)
    doc_total = seg_count * dp_size
    doc_match = all_docs[None, :, :] == jnp.arange(doc_total, dtype=jnp.int32)[:, None, None]
    doc_loglik = jnp.sum(jnp.where(doc_match, seg_loglik[None], 0.0), axis=(1, 2))
    doc_counts = jnp.sum(jnp.where(doc_match, seg_counts[None], 0.0), axis=(1, 2))
    token_logprob = lax.dynamic_slice(
        logprob, (lax.axis_index("dp"), lax.axis_index("seq") * tok_rows), (1, tok_rows)
    )
    return (token_logprob, doc_loglik, doc_counts)


def solution(mesh):
    split = Mesh(
        mesh.devices.reshape(mesh.shape["dp"], mesh.shape["seq"], 4, 2),
        ("dp", "seq", "tensor_0", "tensor_1"),
    )
    in_specs = (
        P(("dp", "seq"), TENSOR),
        P(("dp", "seq"), TENSOR),
        P(("dp", "seq"), TENSOR),
        P(None, TENSOR),
        P(("dp", "seq"), TENSOR),
        P(TENSOR),
        P(TENSOR),
        P(DP_SEQ_TENSOR, None),
        P("dp", "seq"),
        P("dp", None),
        P("dp", None),
        P(),
    )
    out_specs = (P("dp", "seq"), P(), P())
    return jax.shard_map(local, mesh=split, in_specs=in_specs, out_specs=out_specs, check_vma=False)
```

```python
import functools

import jax
import jax.numpy as jnp
from jax import lax
from jax.experimental import pallas as pl
from jax.experimental.pallas import tpu as pltpu
from jax.sharding import Mesh
from jax.sharding import PartitionSpec as P

D = 3584
HEAD_DIM = 256
TENSOR = ("tensor_0", "tensor_1")
DP_SEQ_TENSOR = ("dp", "seq", "tensor_0", "tensor_1")


ATTENTION_CAP = 50.0
LOGIT_CAP = 30.0
EPSILON = 1e-06


def side_by_side(arrays, axis, dim, along):
    ends, at = ([], 0)
    for a in arrays[:-1]:
        at += a.shape[along]
        ends.append(at)
    both = jnp.concatenate(arrays, axis=along)
    return tuple(jnp.split(lax.all_gather(both, axis, axis=dim, tiled=True), ends, axis=along))


def laid_out(blocks, dim):
    blocks = jnp.moveaxis(blocks, 0, dim)
    lengths = blocks.shape
    return blocks.reshape(*lengths[:dim], lengths[dim] * lengths[dim + 1], *lengths[dim + 2 :])


def copy_for_each(shard, axis):
    size = lax.axis_size(axis)
    return lax.all_to_all(
        jnp.broadcast_to(shard[None], (size, *shard.shape)), axis, 0, 0, tiled=True
    )


def collect(shard, axis, dim):
    return laid_out(copy_for_each(shard, axis), dim)


def over_copies(shard, axis):
    return copy_for_each(shard, axis).sum(axis=0)


def together(arrays, axis):
    ends = [0]
    for a in arrays:
        ends.append(ends[-1] + a.size)
    total = over_copies(jnp.concatenate([a.ravel() for a in arrays]), axis)
    return tuple((total[b:e].reshape(a.shape) for a, b, e in zip(arrays, ends, ends[1:])))


def swapped(x):
    return lax.ppermute(x, "tensor_1", [(0, 1), (1, 0)])


def shared_vocabulary(vocab_weight):
    count = vocab_weight.shape[0]
    size, seq_size = lax.axis_size("dp"), lax.axis_size("seq")
    tensor_size = lax.axis_size(TENSOR)
    dp, seq = lax.axis_index("dp"), lax.axis_index("seq")
    place, core = lax.axis_index(TENSOR), lax.axis_index("tensor_1")
    partner = place + 1 - 2 * core
    outward = []
    for x in range(size):
        outward += [(2 * x, 2 * ((x + 1) % size)), (2 * x + 1, 2 * ((x - 1) % size) + 1)]
    near = lax.ppermute(vocab_weight, ("dp", "tensor_1"), outward)

    def first(chip_x, slot):
        return ((chip_x % size * seq_size + seq) * tensor_size + slot) * count

    mine = dp + jnp.where(core == 0, size - 1, 1)
    other = dp + jnp.where(core == 0, 1, size - 1)
    firsts = (first(dp, place), first(dp, partner), first(mine, place), first(other, partner))
    return near, jnp.stack(firsts)


def row_features(hidden, on_first):
    size = lax.axis_size("dp")
    same, cross = [], []
    for x in range(size):
        after, before = (x + 1) % size, (x - 1) % size
        same += [(2 * x, 2 * before), (2 * x + 1, 2 * after + 1)]
        cross += [(2 * x, 2 * after + 1), (2 * x + 1, 2 * before)]
    a = lax.ppermute(hidden, ("dp", "tensor_1"), same)
    b = lax.ppermute(hidden, ("dp", "tensor_1"), cross)
    return jnp.concatenate([jnp.where(on_first, a, b), jnp.where(on_first, b, a)], axis=1)


def moved(x, axis, step):
    size = lax.axis_size(axis)
    return lax.ppermute(x, axis, [(i, (i + step) % size) for i in range(size)])


def row_blocks(block):
    rows, size = block.shape[0], lax.axis_size("seq")
    below = {1: moved(block, "seq", 1), 2: moved(block, "seq", 2)}
    above = {1: moved(block, "seq", -1), 2: moved(block, "seq", -2)}
    for k in range(3, size // 2):
        below[k] = moved(below[k - 1], "seq", 1)
        above[k] = moved(above[k - 1], "seq", -1)
    cut = rows // 16 * 8 + 8
    gap = size // 2 - 2
    head = moved(below[2][:cut], "seq", gap)
    tail = moved(above[2][cut:], "seq", -gap)
    half = range(1, size // 2)
    parts = [block, *[above[k] for k in half], head, tail, *[below[k] for k in half[::-1]]]
    block_of = (lax.axis_index("seq") + jnp.arange(size * rows, dtype=jnp.int32) // rows) % size
    return jnp.concatenate(parts, axis=0), block_of


def ring_step(below, above, axis):
    size = lax.axis_size(axis)
    up = [(i, (i + 1) % size) for i in range(size)]
    down = [(i, (i - 1) % size) for i in range(size)]
    return lax.ppermute(below, axis, up), lax.ppermute(above, axis, down)


def hold_kernel(parts, *refs):
    weights, held, sems = refs[:parts], refs[parts : 2 * parts], refs[2 * parts]
    fills = [
        pltpu.make_async_copy(w, h, sems.at[i]) for i, (w, h) in enumerate(zip(weights, held))
    ]
    for fill in fills:
        fill.start()
    for fill in fills:
        fill.wait()


def on_chip_copies(weights):
    in_place = pl.BlockSpec(memory_space=pl.ANY)
    return pl.pallas_call(
        functools.partial(hold_kernel, len(weights)),
        out_shape=[pltpu.VMEM(w.shape, w.dtype) for w in weights],
        in_specs=[in_place] * len(weights),
        out_specs=[pl.BlockSpec(memory_space=pltpu.VMEM)] * len(weights),
        scratch_shapes=[pltpu.SemaphoreType.DMA((len(weights),))],
        compiler_params=pltpu.CompilerParams(vmem_limit_bytes=2**20),
        cost_estimate=pl.CostEstimate(
            flops=0, transcendentals=0, bytes_accessed=4 * sum(w.size for w in weights)
        ),
        name="on_chip_copies",
    )(*weights)


def block_sums(token_ref, first_ref, labels_ref, weights, ready):
    count = token_ref.shape[0]
    totals = jnp.zeros((1, count), jnp.float32)
    chosen = jnp.zeros((1, count), jnp.float32)
    for i, weight in enumerate(weights):
        ready(i)
        cut = weight.shape[0] // 16 * 8 + 8
        for begin, rows in ((0, cut), (cut, weight.shape[0] - cut)):
            logits = lax.dot_general(
                weight[pl.ds(begin, rows), :],
                token_ref[...],
                (((1,), (1,)), ((), ())),
                preferred_element_type=jnp.float32,
            )
            capped = LOGIT_CAP * jnp.tanh(logits / LOGIT_CAP)
            ids = first_ref[i] + begin + lax.broadcasted_iota(jnp.int32, (rows, count), 0)
            totals += jnp.sum(jnp.exp(capped), axis=0, keepdims=True)
            match = ids == labels_ref[...]
            chosen += jnp.sum(jnp.where(match, capped, 0.0), axis=0, keepdims=True)
    return totals, chosen


def vocabulary_kernel(sizes, resident, parts, first_ref, labels_ref, *refs):
    blocks, weights = refs[: len(sizes)], refs[len(sizes) : len(sizes) + parts]
    out_ref, tokens, sems = refs[len(sizes) + parts :][:3]
    fetched = refs[len(sizes) + parts + 3 :][: parts - resident]
    loads, at = [], 0
    for i, size in enumerate(sizes):
        loads.append(pltpu.make_async_copy(blocks[i], tokens.at[pl.ds(at, size)], sems.at[i]))
        at += size
    fills = [
        pltpu.make_async_copy(weights[resident + i], buffer, refs[-1].at[i])
        for i, buffer in enumerate(fetched)
    ]
    for copy in loads + fills:
        copy.start()
    for load in loads:
        load.wait()

    def ready(i):
        if i >= resident:
            fills[i - resident].wait()

    held = weights[:resident] + fetched
    totals, chosen = block_sums(tokens, first_ref, labels_ref, held, ready)
    out_ref[0:1, :] = totals
    out_ref[1:2, :] = chosen


def vocabulary_sums(blocks, labels, weights, firsts, resident):
    sizes = tuple(b.shape[0] for b in blocks)
    tokens, depth = sum(sizes), blocks[0].shape[1]
    rows = sum(w.shape[0] for w in weights)
    away = weights[resident:]
    in_place = pl.BlockSpec(memory_space=pl.ANY)
    on_chip = pl.BlockSpec(memory_space=pltpu.VMEM)
    return pl.pallas_call(
        functools.partial(vocabulary_kernel, sizes, resident, len(weights)),
        out_shape=jax.ShapeDtypeStruct((2, tokens), jnp.float32),
        in_specs=[
            pl.BlockSpec(memory_space=pltpu.SMEM),
            on_chip,
            *[in_place] * len(sizes),
            *[on_chip] * resident,
            *[in_place] * len(away),
        ],
        out_specs=on_chip,
        scratch_shapes=[
            pltpu.VMEM((tokens, depth), blocks[0].dtype),
            pltpu.SemaphoreType.DMA((len(sizes),)),
            *[pltpu.VMEM(w.shape, w.dtype) for w in away],
            *([pltpu.SemaphoreType.DMA((len(away),))] if away else []),
        ],
        compiler_params=pltpu.CompilerParams(vmem_limit_bytes=(6 + 4 * len(away)) * 2**20),
        cost_estimate=pl.CostEstimate(
            flops=2 * tokens * depth * rows,
            transcendentals=2 * tokens * rows,
            bytes_accessed=2 * (depth * tokens + sum(w.size for w in away)),
        ),
        name="vocabulary_sums",
    )(firsts, labels, *blocks, *weights)


def local(
    query_vectors,
    key_vectors,
    value_vectors,
    out_weight,
    residual,
    post_gain,
    final_gain,
    vocab_weight,
    segment_ids,
    doc_starts,
    doc_index,
    targets,
):
    tok_rows = query_vectors.shape[0]
    seg_row = segment_ids[0]
    starts = doc_starts[0]
    seg_count = starts.shape[0]
    slot_ids = jnp.arange(seg_count, dtype=jnp.int32)
    positions = lax.axis_index("seq") * tok_rows + jnp.arange(tok_rows, dtype=jnp.int32)
    doc_first = jnp.sum(
        jnp.where(slot_ids[:, None] == seg_row[None, :], starts[:, None], 0), axis=0
    )
    local_groups = key_vectors.shape[1] // HEAD_DIM
    group_size = query_vectors.shape[1] // key_vectors.shape[1]
    query_heads = query_vectors.reshape(tok_rows, local_groups, group_size, HEAD_DIM)
    score_scale = HEAD_DIM ** (-0.5)
    kv_width = key_vectors.shape[1]
    kv_block = lax.optimization_barrier(jnp.concatenate((key_vectors, value_vectors), axis=1))
    both, block_of = row_blocks(kv_block)
    near_entries, firsts = shared_vocabulary(vocab_weight)
    key_block, value_block = both[:, :kv_width], both[:, kv_width:]
    row_count = key_block.shape[0]
    key_heads = key_block.reshape(row_count, local_groups, HEAD_DIM)
    value_heads = value_block.reshape(row_count, local_groups, HEAD_DIM)
    raw_scores = jnp.einsum(
        "ikgd,jkd->ikgj", query_heads, key_heads, preferred_element_type=jnp.float32
    )
    capped = ATTENTION_CAP * jnp.tanh(raw_scores * score_scale / ATTENTION_CAP)
    key_positions = block_of * tok_rows + jnp.arange(row_count, dtype=jnp.int32) % tok_rows
    visible = (key_positions[None, :] <= positions[:, None]) & (
        key_positions[None, :] >= doc_first[:, None]
    )
    weights = jnp.where(visible[:, None, None, :], jnp.exp(capped), 0.0)
    rounded = weights.astype(jnp.bfloat16)
    numerator = jnp.einsum(
        "ikgj,jkd->ikgd", rounded, value_heads, preferred_element_type=jnp.float32
    )
    denominator = jnp.sum(weights, axis=-1)
    numerator, denominator = (numerator, denominator)
    attended = (
        (numerator / denominator[..., None])
        .reshape(tok_rows, query_vectors.shape[1])
        .astype(jnp.bfloat16)
    )
    heads = collect(attended, TENSOR, 1)
    branch = jnp.dot(heads, out_weight, preferred_element_type=jnp.float32)
    carried_in = residual.astype(jnp.float32)
    gained = post_gain[None, :] * branch
    sq_branch, sq_carried, cross_sum, sq_gained = together(
        (
            jnp.sum(branch * branch, axis=1),
            jnp.sum(carried_in * carried_in, axis=1),
            jnp.sum(carried_in * gained, axis=1),
            jnp.sum(gained * gained, axis=1),
        ),
        TENSOR,
    )
    inv_branch = 1.0 / jnp.sqrt(sq_branch / D + EPSILON)
    updated = carried_in + gained * inv_branch[:, None]
    sq_total = sq_carried + 2.0 * inv_branch * cross_sum + inv_branch * inv_branch * sq_gained
    hidden = (final_gain[None, :] * updated / jnp.sqrt(sq_total / D + EPSILON)[:, None]).astype(
        jnp.bfloat16
    )
    dp_size = lax.axis_size("dp")
    seq_size = lax.axis_size("seq")
    row_len = tok_rows * seq_size
    on_first = lax.axis_index("tensor_1") == 0
    taken_row = (lax.axis_index("dp") + jnp.where(on_first, 1, dp_size - 1)) % dp_size
    features = collect(row_features(hidden, on_first), "tensor_0", 1)
    features, vocab_weight, near_entries = lax.optimization_barrier(
        (features, vocab_weight, near_entries)
    )
    chip_entries, far_entries = swapped(vocab_weight), swapped(near_entries)
    own_entries = pltpu.with_memory_space_constraint(vocab_weight, pltpu.HBM)
    labels = lax.dynamic_index_in_dim(targets, taken_row, 0, keepdims=False)
    seq_start = lax.axis_index("seq") * tok_rows
    labels = lax.dynamic_slice_in_dim(jnp.concatenate([labels, labels]), seq_start, row_len)
    below, above = [features], [features]
    entries = (own_entries, chip_entries, near_entries, far_entries)
    for step in range(seq_size // 2 - 2):
        below_next, above_next = ring_step(below[-1], above[-1], "seq")
        if step == seq_size // 2 - 3:
            below_next, above_next, held = lax.optimization_barrier(
                (below_next, above_next, on_chip_copies(entries))
            )
        below.append(below_next)
        above.append(above_next)
    near, after = len(above), len(below) - 2
    stay = near * tok_rows
    back = row_len - after * tok_rows
    near_labels = jnp.concatenate([labels[:stay], labels[back:]])
    near_sums = vocabulary_sums(above + below[after:0:-1], near_labels[None], held, firsts, len(held))
    last_below, last_above = ring_step(below[-1], above[-1], "seq")
    last_below, last_above, near_sums, late_entries = lax.optimization_barrier(
        (last_below, last_above, near_sums, entries)
    )
    cut = tok_rows // 16 * 8 + 8
    head, tail = ring_step(last_below[:cut], last_above[cut:], "seq")
    far_blocks = [last_above, head, tail, last_below, below[-1]]
    held = [*on_chip_copies(late_entries[:1]), *late_entries[1:]]
    far_sums = vocabulary_sums(far_blocks, labels[stay:back][None], held, firsts, 1)
    ahead = jnp.concatenate([near_sums[:, :stay], far_sums, near_sums[:, stay:]] * 2, axis=1)
    in_order = lax.dynamic_slice_in_dim(ahead, row_len - seq_start, row_len, axis=1)
    tile = (8, 128)
    spare = jnp.zeros((tile[0] * tile[1] - 2 * row_len,), jnp.float32)
    sent = jnp.concatenate([in_order.ravel(), spare]).reshape(tile)
    by_column = copy_for_each(sent, ("seq", "tensor_1"))
    by_core = jnp.sum(by_column.reshape(seq_size, 2, tile[0] * tile[1]), axis=0)
    packed = jnp.concatenate(
        [
            by_core[:, : 2 * row_len].ravel(),
            starts.astype(jnp.float32),
            doc_index[0].astype(jnp.float32),
            jnp.zeros((2 * (spare.size - seg_count),), jnp.float32),
        ]
    )
    arrived = copy_for_each(packed.reshape(2 * tile[0], tile[1]), ("dp", "tensor_0"))
    arrived = arrived.reshape(dp_size, -1, packed.size)
    by_chip = jnp.sum(arrived[:, :, : 4 * row_len], axis=1)
    segments = arrived[:, 0, 4 * row_len : 4 * row_len + 2 * seg_count].astype(jnp.int32)
    below_rows, above_rows = by_chip[:, : 2 * row_len], by_chip[:, 2 * row_len :]
    complete = jnp.roll(below_rows, 1, axis=0) + jnp.roll(above_rows, -1, axis=0)
    totals, chosen = complete[:, :row_len], complete[:, row_len:]
    all_starts, all_docs = segments[:, :seg_count], segments[:, seg_count:]
    places = jnp.arange(row_len, dtype=jnp.int32)
    ends = jnp.concatenate(
        [all_starts[:, 1:], jnp.full((dp_size, 1), row_len, jnp.int32)], axis=1
    )
    inside = (places[None, None, :] >= all_starts[:, :, None]) & (
        places[None, None, :] < ends[:, :, None]
    )
    last = jnp.sum(jnp.where(inside, ends[:, :, None], 0), axis=1)
    counted = (places[None, :] + 1 < last).astype(jnp.float32)
    logprob = counted * (chosen - jnp.log(totals))
    seg_loglik = jnp.sum(jnp.where(inside, logprob[:, None, :], 0.0), axis=2)
    seg_counts = jnp.sum(jnp.where(inside, counted[:, None, :], 0.0), axis=2)
    doc_total = seg_count * dp_size
    doc_match = all_docs[None, :, :] == jnp.arange(doc_total, dtype=jnp.int32)[:, None, None]
    doc_loglik = jnp.sum(jnp.where(doc_match, seg_loglik[None], 0.0), axis=(1, 2))
    doc_counts = jnp.sum(jnp.where(doc_match, seg_counts[None], 0.0), axis=(1, 2))
    token_logprob = lax.dynamic_slice(
        logprob, (lax.axis_index("dp"), lax.axis_index("seq") * tok_rows), (1, tok_rows)
    )
    return (token_logprob, doc_loglik, doc_counts)


def solution(mesh):
    split = Mesh(
        mesh.devices.reshape(mesh.shape["dp"], mesh.shape["seq"], 4, 2),
        ("dp", "seq", "tensor_0", "tensor_1"),
    )
    in_specs = (
        P(("dp", "seq"), TENSOR),
        P(("dp", "seq"), TENSOR),
        P(("dp", "seq"), TENSOR),
        P(None, TENSOR),
        P(("dp", "seq"), TENSOR),
        P(TENSOR),
        P(TENSOR),
        P(DP_SEQ_TENSOR, None),
        P("dp", "seq"),
        P("dp", None),
        P("dp", None),
        P(),
    )
    out_specs = (P("dp", "seq"), P(), P())
    return jax.shard_map(local, mesh=split, in_specs=in_specs, out_specs=out_specs, check_vma=False)
```
